32 devices in a mesh: men: 16 (over z, x, core), women: 2 (over y).
Axes of the slice: x: 2, y: 2, z: 4, core: 2. Of those that a mesh axis runs over, the one named last changes fastest.
Arguments:
- men_traits: bfloat16 [64, 16384], P(None, ('men', 'women')), may hold values from -4 to 4
- women_traits: bfloat16 [64, 8192], P(None, ('women', 'men')), may hold values from -4 to 4
- affinity: float32 [64, 64], replicated, may hold values from -0.375 to 0.375
- observed: float32 [64, 64], replicated, may hold values from -0.25 to 0.25
- men_mass: float32 [16384], P('men'), may hold values from 0.5 to 2
- women_mass: float32 [8192], P('women'), may hold values from 0.5 to 2
Outputs:
- men_scale: float32 [16384], P('men')
- women_scale: float32 [8192], P('women')
- updated: float32 [64, 64], replicated
The draws below stay inside these ranges and needn't reach their ends.
All inputs are finite; a program needn't handle non-finite values.
Results may differ from the reference program's by a relative error of at most 0.0022.
Values may be sent and summed in bfloat16 or wider, within the bound.
A program may use at most 64 MiB of HBM per device.

```python
import math
import jax
import jax.numpy as jnp
from jax import lax

K = 64
M_DEV = 1024
W_DEV = 4096
ITERS = 2
NM = 16384
NW = 8192


def men_levels(key):
    block_count = NM // M_DEV
    return jax.random.uniform(jax.random.fold_in(key, 101), (K, block_count), jnp.float32, -1.0, 0.6)


def trait_noise(key, columns):
    return jax.random.truncated_normal(key, -2.9, 2.9, (K, columns), jnp.float32)


def draw_men_traits(key, part):
    levels = men_levels(key)
    spread_levels = jnp.repeat(levels, M_DEV, axis=1, total_repeat_length=NM)
    noise = trait_noise(jax.random.fold_in(key, 102), NM)
    values = jnp.clip(spread_levels + noise, -4.0, 4.0)
    return values.astype(jnp.bfloat16)


def draw_men_mass(key, part):
    levels = men_levels(key)
    block_log = 0.5 * (levels[0] + 0.2) / 0.8
    spread_log = jnp.repeat(block_log, M_DEV, total_repeat_length=NM)
    noise = jax.random.uniform(jax.random.fold_in(key, 103), (NM,), jnp.float32, -0.18, 0.18)
    values = jnp.clip(jnp.exp(spread_log + noise), 0.5, 2.0)
    return values.astype(jnp.float32)


def draw_women_traits(key, part):
    block_count = NW // W_DEV
    levels = jax.random.uniform(jax.random.fold_in(key, 201), (K, block_count), jnp.float32, -0.4, 0.8)
    spread_levels = jnp.repeat(levels, W_DEV, axis=1, total_repeat_length=NW)
    noise = trait_noise(jax.random.fold_in(key, 202), NW)
    values = jnp.clip(spread_levels + noise, -4.0, 4.0)
    return values.astype(jnp.bfloat16)


def level_of(rng, dims, split, least, top_value):
    loudness, own = 1.0, jax.random.fold_in(rng, 6)
    for dim, parts in split:
        steps = jnp.exp(jax.random.uniform(jax.random.fold_in(own, dim), (parts,), jnp.float32, least / len(split), top_value / len(split)))
        loudness = loudness * jnp.repeat(steps, dims[dim] // parts).reshape([-1 if axis == dim else 1 for axis in range(len(dims))])
    return loudness


def bell_draw(rng, shape, scale, reach, held_as=jnp.bfloat16):
    drawn = jax.random.normal(rng, shape, jnp.float32) * scale
    return jnp.minimum(jnp.maximum(drawn, -reach), reach).astype(held_as)


def setup_inputs(seed: int = 0) -> dict:
    splits = jax.random.split(jax.random.key(seed), 7)
    return {
        "men_traits": draw_men_traits(jax.random.fold_in(splits[6], 71), 0),
        "women_traits": draw_women_traits(jax.random.fold_in(splits[6], 71), 0),
        "affinity": bell_draw(splits[2], (K, K), 0.025, 0.375, jnp.float32),
        "observed": bell_draw(splits[3], (K, K), 0.015625, 0.25, jnp.float32),
        "men_mass": draw_men_mass(jax.random.fold_in(splits[6], 71), 0),
        "women_mass": jnp.clip(jnp.exp(math.log(2.0) - 1.3862944 * jax.random.uniform(splits[5], (NW,), jnp.float32) ** level_of(splits[5], (NW,), ((0, 2),), -0.2, 0.2)), 0.5, 2.0),
    }


HIGH = lax.Precision.HIGHEST


def kernel_rows(scaled_block, women_traits, women_count):
    surplus = lax.dot_general(scaled_block, women_traits, (((0,), (0,)), ((), ())), preferred_element_type=jnp.float32)
    return jnp.exp(surplus) / women_count


def reference(men_traits, women_traits, affinity, observed, men_mass, women_mass):
    traits = men_traits.shape[0]
    men_total = men_traits.shape[1]
    women_total = women_traits.shape[1]
    women_count = float(women_total)
    block_rows = math.gcd(men_total, 1024)
    block_count = men_total // block_rows
    men_float = men_traits.astype(jnp.float32)
    scaled = jnp.dot(affinity.T, men_float, precision=HIGH).astype(jnp.bfloat16)
    scaled_blocks = scaled.reshape(traits, block_count, block_rows).transpose(1, 0, 2)
    men_blocks = men_float.reshape(traits, block_count, block_rows).transpose(1, 0, 2)
    women_float = women_traits.astype(jnp.float32)

    def rows_of(women_scale):
        def one_block(scaled_block):
            return jnp.dot(kernel_rows(scaled_block, women_traits, women_count), women_scale, precision=HIGH)
        return lax.map(one_block, scaled_blocks).reshape(men_total)

    def cols_of(men_scale):
        scale_blocks = men_scale.reshape(block_count, block_rows)

        def one_block(total, pieces):
            kernel = kernel_rows(pieces[0], women_traits, women_count)
            return total + jnp.dot(pieces[1], kernel, precision=HIGH), None
        total, _ = lax.scan(one_block, jnp.zeros((women_total,), jnp.float32), (scaled_blocks, scale_blocks))
        return total

    women_scale = jnp.ones((women_total,), jnp.float32)
    men_scale = men_mass
    for round_index in range(ITERS):
        men_scale = men_mass / rows_of(women_scale)
        women_scale = women_mass / cols_of(men_scale)

    scale_blocks = men_scale.reshape(block_count, block_rows)

    def moment_block(total, pieces):
        kernel = kernel_rows(pieces[0], women_traits, women_count)
        plan = pieces[1][:, None] * kernel * women_scale[None, :]
        inner = jnp.dot(plan, women_float.T, precision=HIGH)
        return total + jnp.dot(pieces[2], inner, precision=HIGH), None

    moment, _ = lax.scan(moment_block, jnp.zeros((traits, traits), jnp.float32), (scaled_blocks, scale_blocks, men_blocks))
    updated = affinity + observed - moment / float(men_total)
    return men_scale, women_scale, updated
```

```python
import functools
import math
import jax
import jax.numpy as jnp
import ml_dtypes
import numpy as np
from jax import lax
from jax.experimental import pallas as pl
from jax.experimental.pallas import tpu as pltpu
from jax.sharding import PartitionSpec as P

F32, BF16 = jnp.float32, jnp.bfloat16
MESH = pl.DeviceIdType.MESH
LHS_T = (((0,), (0,)), ((), ()))
RHS_T = (((1,), (1,)), ((), ()))


def split3(value):
    high = value.astype(BF16)
    rest = value - high.astype(F32)
    mid = rest.astype(BF16)
    low = (rest - mid.astype(F32)).astype(BF16)
    return high, mid, low


def factors(men):
    cores = 2 if men % 2 == 0 else 1
    chips = men // cores
    planes = 1 << (chips.bit_length() // 2)
    if chips % planes:
        planes = 1
    return planes, chips // planes, cores


def body(dims, ws, men_total, women_total,
         men_ref, women_ref, aff_hbm, obs_hbm, mm_hbm, wm_hbm,
         ms_out, ws_out, up_out,
         men_buf, wom_buf, scaled_ref, e_ref, t_ref, col_ref, rsum_ref, scale_ref,
         aff_ref, obs_ref, wm_ref, mass_buf, wx_buf,
         r_buf, c_buf, mxy_buf, mc_buf, mz_buf,
         own_sem, gm_s, gm_r, gz_s, gz_r, gc_s, gc_r, mm_s, mm_r, wx_s, wx_r,
         rx_s, rx_r, cz_s, cz_r, mc_s, mc_r, mz_s, mz_r):
    zs, xs, cs = dims
    nm, nb = xs * ws, zs * cs
    traits, wb = women_ref.shape
    deep = wom_buf.shape[1]
    mb = men_ref.shape[1]
    rows = mm_hbm.shape[1]
    group_rows = nm * mb
    log_count = math.log(women_total)
    mi = lax.axis_index("men")
    yi = lax.axis_index("women")
    ci = lax.rem(mi, cs)
    xi = lax.rem(lax.div(mi, cs), xs)
    zi = lax.div(mi, cs * xs)
    xy_me = xi * ws + yi
    zc_me = ci * zs + zi

    def plus(value, step, size):
        return lax.rem(value + step, size)

    def xy_peer(dx, dy):
        return ((zi * xs + plus(xi, dx, xs)) * cs + ci, plus(yi, dy, ws))

    def zc_peer(dc, dz):
        return ((plus(zi, dz, zs) * xs + xi) * cs + plus(ci, dc, cs), yi)

    def traits_of(q):
        return wom_buf.at[q, pl.ds(0, traits)]

    xy_ids = [xy_peer(dx, dy) for dx in range(xs) for dy in range(ws) if dx + dy]
    zc_ids = [zc_peer(dc, dz) for dc in range(cs) for dz in range(zs) if dc + dz]
    x_ids = [xy_peer(dx, 0) for dx in range(1, xs)]
    c_ids = [zc_peer(dc, 0) for dc in range(1, cs)]
    z_ids = [zc_peer(0, dz) for dz in range(1, zs)]

    barrier = pltpu.get_barrier_semaphore()
    everyone = xy_ids + zc_ids
    for peer in everyone:
        pl.semaphore_signal(barrier, inc=1, device_id=peer, device_id_type=MESH)
    local = [
        pltpu.make_async_copy(src, dst, own_sem.at[k])
        for k, (src, dst) in enumerate([
            (men_ref, men_buf.at[xy_me]), (women_ref, traits_of(zc_me)), (aff_hbm, aff_ref),
            (mm_hbm, mass_buf.at[xi]), (wm_hbm, wm_ref), (obs_hbm, obs_ref)])
    ]
    for copy in local:
        copy.start()
    def remote(src, dst, send, recv, peer):
        return pltpu.make_async_remote_copy(
            src_ref=src, dst_ref=dst, send_sem=send, recv_sem=recv,
            device_id=peer, device_id_type=MESH)

    def z_copy(dz):
        return remote(women_ref, traits_of(zc_me), gz_s.at[dz], gz_r.at[dz], zc_peer(0, dz))

    def source_z(dz):
        return plus(zi, zs - dz, zs)

    def c_copy(dz):
        held = traits_of(ci * zs + source_z(dz))
        return remote(held, held, gc_s.at[dz], gc_r.at[dz], zc_peer(1, 0))

    def m_copy(k):
        return remote(men_ref, men_buf.at[xy_me], gm_s.at[k], gm_r.at[k],
                      xy_peer(lax.div(k, ws), lax.rem(k, ws)))

    def shard_of(k):
        return plus(xi, xs - lax.div(k, ws), xs) * ws + plus(yi, ws - lax.rem(k, ws), ws)

    def rows_of(shard):
        return pl.ds(pl.multiple_of(shard * mb, mb), mb)

    column = lax.broadcasted_iota(jnp.int32, (1, deep), 1)
    ones_row = jnp.where((column >= traits) & (column < traits + 3), 1.0, 0.0).astype(F32)
    line = lax.broadcasted_iota(jnp.int32, (deep - traits, wb), 0)
    tail = jnp.zeros((deep - traits, wb), F32)
    rest = log_count
    for step in range(3):
        piece = float(np.asarray(rest, ml_dtypes.bfloat16))
        tail = jnp.where(line == step, -piece, tail)
        rest -= piece
    tail = tail.astype(BF16)
    for q in range(nb):
        wom_buf[q, traits:] = tail
    rsum_ref[...] = jnp.zeros_like(rsum_ref)
    tile = math.gcd(mb, 256)
    fold = wb // 128 if wb % 128 == 0 else 1
    lanes = wb // fold

    def make_scaled(shard):
        wide = jnp.concatenate([aff_ref[...], jnp.zeros((traits, deep - traits), F32)], axis=1)
        high, mid, low = [
            lax.dot_general(men_buf[shard], part, LHS_T, preferred_element_type=F32)
            for part in split3(wide)
        ]
        scaled_ref[rows_of(shard), :] = (((low + mid) + high) + ones_row).astype(BF16)

    def fill(blocks, start, count):
        for part in range(count):
            at = pl.ds(pl.multiple_of(start + part * tile, tile), tile)
            total = None
            for q in blocks:
                surplus = jnp.dot(scaled_ref[at, :], wom_buf[q], preferred_element_type=F32)
                kernel = jnp.exp(surplus)
                e_ref[q, at, :] = kernel.astype(BF16)
                for piece in range(fold):
                    term = kernel[:, piece * lanes:(piece + 1) * lanes]
                    total = term if total is None else total + term
            rsum_ref[at, :] += total

    def fill_men(blocks, ks):
        for k in ks:
            fill(blocks, shard_of(k) * mb, mb // tile)

    for copy in local:
        copy.wait()
    make_scaled(xy_me)
    fill([zc_me], xy_me * mb, mb // tile)

    pl.semaphore_wait(barrier, len(everyone))
    if cs > 1:
        c_copy(0).start()
    for dz in range(1, zs):
        z_copy(dz).start()
    for k in range(1, nm):
        m_copy(k).start()
    pending = []
    for k, peer in enumerate(x_ids):
        copy = remote(mm_hbm, mass_buf.at[xi], mm_s.at[k], mm_r.at[k], peer)
        copy.start()
        pending.append(copy)
    mass_copies = list(pending)

    def step_of(n):
        near = [sorted(range(zs), key=lambda z: (abs(z - own), -z))[n] for own in range(zs)]
        steps = [(own - z) % zs for own, z in enumerate(near)]
        value = jnp.int32(steps[0])
        for own in range(1, zs):
            value = jnp.where(zi == own, steps[own], value)
        return value

    def own_block(n):
        return ci * zs + source_z(order[n])

    def twin_block(n):
        return plus(ci, 1, cs) * zs + source_z(order[n])

    order = [0] + [step_of(n) for n in range(1, zs)]
    if cs == 2 and nm == 4 and zs == 4:
        def take_z(n):
            z_copy(order[n]).wait_recv()
            c_copy(order[n]).start()

        def take_men(k):
            m_copy(k).wait_recv()
            make_scaled(shard_of(k))

        c_copy(0).wait_recv()
        fill_men([twin_block(0)], [0])
        take_z(1)
        fill_men([own_block(1)], [0])
        take_men(1)
        fill_men([own_block(0), twin_block(0), own_block(1)], [1])
        take_z(2)
        c_copy(order[1]).wait_recv()
        fill_men([twin_block(1)], [0, 1])
        take_men(2)
        fill_men([own_block(0), twin_block(0), own_block(1), twin_block(1)], [2])
        take_z(3)
        fill_men([own_block(2)], [0, 1, 2])
        take_men(3)
        fill_men([own_block(0), twin_block(0), own_block(1), twin_block(1), own_block(2)], [3])
        c_copy(order[2]).wait_recv()
        fill([twin_block(2), own_block(3)], 0, group_rows // tile)
        c_copy(order[3]).wait_recv()
        fill([twin_block(3)], 0, group_rows // tile)
    else:
        def own_men(dz, carry):
            z_copy(dz).wait_recv()
            if cs > 1:
                c_copy(dz).start()
            fill([ci * zs + source_z(dz)], xy_me * mb, mb // tile)
            return carry

        def other_men(k, carry):
            m_copy(k).wait_recv()
            shard = shard_of(k)
            make_scaled(shard)
            for z in range(zs):
                fill([ci * zs + z], shard * mb, mb // tile)
            return carry

        def other_core(dz, carry):
            c_copy(dz).wait_recv()
            fill([plus(ci, 1, cs) * zs + source_z(dz)], 0, group_rows // tile)
            return carry

        lax.fori_loop(1, zs, own_men, 0)
        lax.fori_loop(1, nm, other_men, 0)
        if cs > 1:
            lax.fori_loop(0, zs, other_core, 0)

    def group_sum(value, buf, me, send, recv, peers):
        if not peers:
            return value
        buf[me] = value
        copies = []
        for k, peer in enumerate(peers):
            copy = remote(buf.at[me], buf.at[me], send.at[k], recv.at[k], peer)
            copy.start()
            copies.append(copy)
        for copy in copies:
            copy.wait_recv()
        pending.extend(copies)
        total = buf[0]
        for slot in range(1, buf.shape[0]):
            total = total + buf[slot]
        return total

    for copy in mass_copies:
        copy.wait_recv()
    men_mass = jnp.concatenate([mass_buf[x] for x in range(xs)], axis=1)
    men_full = jnp.concatenate([men_buf[k] for k in range(nm)], axis=1)
    mass_q = None
    for x in range(xs):
        order = [(z * xs + x) * cs + c for c in range(cs) for z in range(zs)]
        mine = jnp.concatenate([wm_ref[:, p * wb:(p + 1) * wb] for p in order], axis=0)
        mass_q = mine if mass_q is None else jnp.where(xi == x, mine, mass_q)

    def men_update(it, row_sum):
        return men_mass / group_sum(row_sum, r_buf.at[it], xy_me, rx_s.at[it], rx_r.at[it], xy_ids)

    def women_update(it, partial):
        return mass_q / group_sum(partial, c_buf.at[it], zc_me, cz_s.at[it], cz_r.at[it], zc_ids)

    zeros13 = jnp.zeros((13, group_rows), BF16)
    zeros13w = jnp.zeros((13, wb), BF16)

    def sweep(step, carry):
        for q in range(nb):
            carry = step(q, carry)
        return carry

    sums = rsum_ref[...]
    high = sums.astype(BF16)
    low = (sums - high.astype(F32)).astype(BF16)
    total = lax.dot_general(jnp.ones((16, 2 * lanes), BF16), jnp.concatenate([high, low], axis=1),
                            RHS_T, preferred_element_type=F32)
    scale = men_update(0, total[0:1])
    left0 = jnp.concatenate(list(split3(scale)) + [zeros13], axis=0)

    def col_step(q, carry):
        out = jnp.dot(left0, e_ref[q], preferred_element_type=F32)
        col_ref[q:q + 1, :] = out[0:1] + out[1:2] + out[2:3]
        return carry

    sweep(col_step, 0)
    col_ref[...] = women_update(0, col_ref[...])

    def row_step(q, total):
        lines = jnp.concatenate(list(split3(col_ref[q:q + 1, :])) + [zeros13w], axis=0)
        return total + lax.dot_general(lines, e_ref[q], RHS_T, preferred_element_type=F32)

    total = sweep(row_step, jnp.zeros((16, group_rows), F32))
    scale = men_update(1, total[0:1] + total[1:2] + total[2:3])
    for x in range(xs):
        scale_ref[x] = scale[:, x * rows:(x + 1) * rows]
    ms_out[...] = scale_ref[xi]

    weighted = (men_full.astype(F32) * scale).astype(BF16)
    left = jnp.concatenate([weighted] + list(split3(scale)) + [zeros13], axis=0)

    def both_step(q, carry):
        out = jnp.dot(left, e_ref[q], preferred_element_type=F32)
        t_ref[q] = out[0:traits]
        col_ref[q:q + 1, :] = (out[traits:traits + 1] + out[traits + 1:traits + 2]
                               + out[traits + 2:traits + 3])
        return carry

    sweep(both_step, 0)
    women_scale = women_update(1, col_ref[...])
    col_ref[...] = women_scale
    wx_buf[xi] = women_scale
    wx_copies = []
    for k, peer in enumerate(x_ids):
        copy = remote(wx_buf.at[xi], wx_buf.at[xi], wx_s.at[k], wx_r.at[k], peer)
        copy.start()
        wx_copies.append(copy)
    pending.extend(wx_copies)

    def moment_step(q, moment):
        inner = t_ref[q] * col_ref[q:q + 1, :]
        high = inner.astype(BF16)
        low = (inner - high.astype(F32)).astype(BF16)
        both = jnp.concatenate([high, low], axis=0)
        return moment + lax.dot_general(both, wom_buf[q, 0:traits], RHS_T, preferred_element_type=F32)

    moment = sweep(moment_step, jnp.zeros((2 * traits, traits), F32))
    moment = moment[0:traits] + moment[traits:]
    half = traits // 2
    packed = jnp.concatenate([moment[0:half], moment[half:]], axis=1)
    packed = group_sum(packed, mxy_buf, xy_me, rx_s.at[2], rx_r.at[2], xy_ids)
    packed = group_sum(packed, mc_buf, ci, mc_s, mc_r, c_ids)
    for copy in wx_copies:
        copy.wait_recv()
    for x in range(xs):
        scales = wx_buf[x]
        for q in range(nb):
            p = ((q % zs) * xs + x) * cs + q // zs
            ws_out[:, p * wb:(p + 1) * wb] = scales[q:q + 1, :]
    packed = group_sum(packed, mz_buf, zi, mz_s, mz_r, z_ids)
    moment = jnp.concatenate([packed[:, 0:traits], packed[:, traits:]], axis=0)
    up_out[...] = aff_ref[...] + obs_ref[...] - moment * (1.0 / men_total)

    for copy in pending:
        copy.wait_send()
    for dz in range(1, zs):
        z_copy(dz).wait_send()
    for k in range(1, nm):
        m_copy(k).wait_send()
    if cs > 1:
        for dz in range(zs):
            c_copy(dz).wait_send()


def deliver(ms_ref, ws_ref, up_ref, ms_out, ws_out, up_out, sems):
    copies = [
        pltpu.make_async_copy(src, dst, sems.at[k])
        for k, (src, dst) in enumerate([(ms_ref, ms_out), (ws_ref, ws_out), (up_ref, up_out)])
    ]
    for copy in copies:
        copy.start()
    for copy in copies:
        copy.wait()


def solution(mesh):
    men_axis, women_axis = mesh.shape["men"], mesh.shape["women"]
    dims = factors(men_axis)
    zs, xs, cs = dims

    def on_device(men_traits, women_traits, affinity, observed, men_mass, women_mass):
        traits, mb = men_traits.shape
        wb = women_traits.shape[1]
        rows, cols = men_mass.shape[0], women_mass.shape[0]
        nm, nb = xs * women_axis, zs * cs
        deep = traits + 16
        dma = pltpu.SemaphoreType.DMA
        vmem = pl.BlockSpec(memory_space=pltpu.VMEM)
        anywhere = pl.BlockSpec(memory_space=pl.ANY)
        packed = (traits // 2, 2 * traits)
        out = pl.pallas_call(
            functools.partial(body, dims, women_axis, rows * men_axis, cols * women_axis),
            out_shape=(
                pltpu.VMEM((1, rows), F32),
                pltpu.VMEM((1, cols), F32),
                pltpu.VMEM((traits, traits), F32),
            ),
            in_specs=[anywhere] * 6,
            out_specs=(vmem, vmem, vmem),
            scratch_shapes=[
                pltpu.VMEM((nm, traits, mb), BF16),
                pltpu.VMEM((nb, deep, wb), BF16),
                pltpu.VMEM((nm * mb, deep), BF16),
                pltpu.VMEM((nb, nm * mb, wb), BF16),
                pltpu.VMEM((nb, traits, wb), F32),
                pltpu.VMEM((nb, wb), F32),
                pltpu.VMEM((nm * mb, wb if wb % 128 else 128), F32),
                pltpu.VMEM((xs, 1, rows), F32),
                pltpu.VMEM((traits, traits), F32),
                pltpu.VMEM((traits, traits), F32),
                pltpu.VMEM((1, cols), F32),
                pltpu.VMEM((xs, 1, rows), F32),
                pltpu.VMEM((xs, nb, wb), F32),
                pltpu.VMEM((2, nm, 1, nm * mb), F32),
                pltpu.VMEM((2, nb, nb, wb), F32),
                pltpu.VMEM((nm,) + packed, F32),
                pltpu.VMEM((cs,) + packed, F32),
                pltpu.VMEM((zs,) + packed, F32),
                dma((6,)),
                dma((nm,)), dma((nm,)),
                dma((zs,)), dma((zs,)),
                dma((zs,)), dma((zs,)),
                dma((xs,)), dma((xs,)),
                dma((xs,)), dma((xs,)),
                dma((3, nm)), dma((3, nm)),
                dma((2, nb)), dma((2, nb)),
                dma((cs,)), dma((cs,)),
                dma((zs,)), dma((zs,)),
            ],
            compiler_params=pltpu.CompilerParams(
                collective_id=0, has_side_effects=True, vmem_limit_bytes=60 * 1024 * 1024),
        )(men_traits, women_traits, affinity, observed,
          men_mass.reshape(1, rows), women_mass.reshape(1, cols))
        out = pl.pallas_call(
            deliver,
            out_shape=(
                jax.ShapeDtypeStruct((1, rows), F32),
                jax.ShapeDtypeStruct((1, cols), F32),
                jax.ShapeDtypeStruct((traits, traits), F32),
            ),
            in_specs=[vmem] * 3,
            out_specs=(anywhere,) * 3,
            scratch_shapes=[dma((3,))],
        )(*[pltpu.with_memory_space_constraint(value, pltpu.VMEM) for value in out])
        return out[0].reshape(rows), out[1].reshape(cols), out[2]

    placed = (P(None, ("men", "women")), P(None, ("women", "men")), P(), P(), P("men"), P("women"))
    return jax.shard_map(
        on_device,
        mesh=mesh,
        in_specs=placed,
        out_specs=(P("men"), P("women"), P()),
        check_vma=False,
    )
```

```python
import functools
import math
import jax
import jax.numpy as jnp
import ml_dtypes
import numpy as np
from jax import lax
from jax.experimental import pallas as pl
from jax.experimental.pallas import tpu as pltpu
from jax.sharding import PartitionSpec as P

F32, BF16 = jnp.float32, jnp.bfloat16
MESH = pl.DeviceIdType.MESH
LHS_T = (((0,), (0,)), ((), ()))
RHS_T = (((1,), (1,)), ((), ()))


def split3(value):
    high = value.astype(BF16)
    rest = value - high.astype(F32)
    mid = rest.astype(BF16)
    low = (rest - mid.astype(F32)).astype(BF16)
    return high, mid, low


def factors(men):
    cores = 2 if men % 2 == 0 else 1
    chips = men // cores
    planes = 1 << (chips.bit_length() // 2)
    if chips % planes:
        planes = 1
    return planes, chips // planes, cores


def body(dims, ws, men_total, women_total,
         men_ref, women_ref, aff_hbm, obs_hbm, mm_hbm, wm_hbm,
         ms_out, ws_out, up_out,
         men_buf, wom_buf, scaled_ref, e_ref, t_ref, col_ref, rsum_ref, scale_ref,
         left_aff, aff_ref, obs_ref, wm_ref, mass_buf, wx_buf,
         r_buf, c_buf, mxy_buf, mz_buf, t_in,
         own_sem, gm_s, gm_r, gz_s, gz_r, gc_s, gc_r, mm_s, mm_r, wx_s, wx_r,
         rx_s, rx_r, cz_s, cz_r, tx_s, tx_r, mz_s, mz_r):
    zs, xs, cs = dims
    nm, nb = xs * ws, zs * cs
    traits, wb = women_ref.shape
    deep = wom_buf.shape[1]
    mb = men_ref.shape[1]
    rows = mm_hbm.shape[1]
    group_rows = nm * mb
    log_count = math.log(women_total)
    mi = lax.axis_index("men")
    yi = lax.axis_index("women")
    ci = lax.rem(mi, cs)
    xi = lax.rem(lax.div(mi, cs), xs)
    zi = lax.div(mi, cs * xs)
    xy_me = xi * ws + yi
    zc_me = ci * zs + zi

    def plus(value, step, size):
        return lax.rem(value + step, size)

    def xy_peer(dx, dy):
        return ((zi * xs + plus(xi, dx, xs)) * cs + ci, plus(yi, dy, ws))

    def zc_peer(dc, dz):
        return ((plus(zi, dz, zs) * xs + xi) * cs + plus(ci, dc, cs), yi)

    def traits_of(q):
        return wom_buf.at[q, pl.ds(0, traits)]

    xy_ids = [xy_peer(dx, dy) for dx in range(xs) for dy in range(ws) if dx + dy]
    zc_ids = [zc_peer(dc, dz) for dc in range(cs) for dz in range(zs) if dc + dz]
    x_ids = [xy_peer(dx, 0) for dx in range(1, xs)]

    barrier = pltpu.get_barrier_semaphore()
    everyone = xy_ids + zc_ids
    for peer in everyone:
        pl.semaphore_signal(barrier, inc=1, device_id=peer, device_id_type=MESH)
    local = [
        pltpu.make_async_copy(src, dst, own_sem.at[k])
        for k, (src, dst) in enumerate([
            (men_ref, men_buf.at[xy_me]), (women_ref, traits_of(zc_me)), (aff_hbm, aff_ref),
            (mm_hbm, mass_buf.at[xi]), (wm_hbm, wm_ref), (obs_hbm, obs_ref)])
    ]
    for copy in local:
        copy.start()
    def remote(src, dst, send, recv, peer):
        return pltpu.make_async_remote_copy(
            src_ref=src, dst_ref=dst, send_sem=send, recv_sem=recv,
            device_id=peer, device_id_type=MESH)

    def z_copy(dz):
        return remote(women_ref, traits_of(zc_me), gz_s.at[dz], gz_r.at[dz], zc_peer(0, dz))

    def source_z(dz):
        return plus(zi, zs - dz, zs)

    def c_copy(dz):
        held = traits_of(ci * zs + source_z(dz))
        return remote(held, held, gc_s.at[dz], gc_r.at[dz], zc_peer(1, 0))

    def m_copy(k):
        return remote(men_ref, men_buf.at[xy_me], gm_s.at[k], gm_r.at[k],
                      xy_peer(lax.div(k, ws), lax.rem(k, ws)))

    def by_distance(sign):
        order = [0]
        for n in range(1, zs):
            near = [sorted(range(zs), key=lambda z: (abs(z - own), -z))[n] for own in range(zs)]
            steps = [sign * (z - own) % zs for own, z in enumerate(near)]
            value = jnp.int32(steps[0])
            for own in range(1, zs):
                value = jnp.where(zi == own, steps[own], value)
            order.append(value)
        return order

    order, send_order = by_distance(-1), by_distance(1)
    first_copy = remote(women_ref, traits_of(zc_me), gc_s.at[0], gc_r.at[0], zc_peer(1, 0)) if cs > 1 else None
    pl.semaphore_wait(barrier, len(everyone))
    if cs > 1:
        first_copy.start()
    for n in range(1, zs):
        z_copy(send_order[n]).start()
    for k in range(1, nm):
        m_copy(k).start()
    pending = []
    for k, peer in enumerate(x_ids):
        copy = remote(mm_hbm, mass_buf.at[xi], mm_s.at[k], mm_r.at[k], peer)
        copy.start()
        pending.append(copy)
    mass_copies = list(pending)

    def shard_of(k):
        return plus(xi, xs - lax.div(k, ws), xs) * ws + plus(yi, ws - lax.rem(k, ws), ws)

    def rows_of(shard):
        return pl.ds(pl.multiple_of(shard * mb, mb), mb)

    tile = math.gcd(mb, 256)
    fold = wb // 128 if wb % 128 == 0 else 1
    lanes = wb // fold

    def make_scaled(shard):
        block = men_buf[shard]
        tall = jnp.dot(left_aff[...], jnp.concatenate([block] * 3, axis=0), preferred_element_type=F32)
        scaled_ref[rows_of(shard), :] = jnp.transpose(tall + ones_column).astype(BF16)

    def fill(blocks, start, count):
        for part in range(count):
            at = pl.ds(pl.multiple_of(start + part * tile, tile), tile)
            total = None
            for q in blocks:
                surplus = jnp.dot(scaled_ref[at, :], wom_buf[q], preferred_element_type=F32)
                kernel = jnp.exp(surplus)
                e_ref[q, at, :] = kernel.astype(BF16)
                for piece in range(fold):
                    term = kernel[:, piece * lanes:(piece + 1) * lanes]
                    total = term if total is None else total + term
            rsum_ref[at, :] += total

    def fill_men(blocks, ks):
        for k in ks:
            fill(blocks, shard_of(k) * mb, mb // tile)

    place = lax.broadcasted_iota(jnp.int32, (deep, 1), 0)
    ones_column = jnp.where((place >= traits) & (place < traits + 3), 1.0, 0.0).astype(F32)
    line = lax.broadcasted_iota(jnp.int32, (deep - traits, wb), 0)
    tail = jnp.zeros((deep - traits, wb), F32)
    rest = log_count
    for step in range(3):
        piece = float(np.asarray(rest, ml_dtypes.bfloat16))
        tail = jnp.where(line == step, -piece, tail)
        rest -= piece
    tail = tail.astype(BF16)
    for q in range(nb):
        wom_buf[q, traits:] = tail
    rsum_ref[...] = jnp.zeros_like(rsum_ref)
    for copy in local:
        copy.wait()
    wide = jnp.concatenate(split3(jnp.transpose(aff_ref[...])), axis=1)
    left_aff[...] = jnp.concatenate([wide, jnp.zeros((deep - traits, 3 * traits), BF16)], axis=0)
    make_scaled(xy_me)
    fill([zc_me], xy_me * mb, mb // tile)

    def own_block(n):
        return ci * zs + source_z(order[n])

    def twin_block(n):
        return plus(ci, 1, cs) * zs + source_z(order[n])

    if cs == 2 and nm == 4 and zs == 4:
        def take_z(n):
            z_copy(order[n]).wait_recv()
            c_copy(order[n]).start()

        def take_men(k):
            m_copy(k).wait_recv()
            make_scaled(shard_of(k))

        c_copy(0).wait_recv()
        fill_men([twin_block(0)], [0])
        take_z(1)
        fill_men([own_block(1)], [0])
        take_men(2)
        fill_men([own_block(0), twin_block(0), own_block(1)], [2])
        take_z(2)
        c_copy(order[1]).wait_recv()
        fill_men([twin_block(1)], [0, 2])
        take_men(1)
        fill_men([own_block(0), twin_block(0), own_block(1), twin_block(1)], [1])
        take_z(3)
        fill_men([own_block(2)], [0, 1, 2])
        take_men(3)
        fill_men([own_block(0), twin_block(0), own_block(1), twin_block(1), own_block(2)], [3])
        c_copy(order[2]).wait_recv()
        fill([twin_block(2), own_block(3)], 0, group_rows // tile)
        c_copy(order[3]).wait_recv()
        fill([twin_block(3)], 0, group_rows // tile)
    else:
        def own_men(dz, carry):
            z_copy(dz).wait_recv()
            if cs > 1:
                c_copy(dz).start()
            fill([ci * zs + source_z(dz)], xy_me * mb, mb // tile)
            return carry

        def other_men(k, carry):
            m_copy(k).wait_recv()
            shard = shard_of(k)
            make_scaled(shard)
            for z in range(zs):
                fill([ci * zs + z], shard * mb, mb // tile)
            return carry

        def other_core(dz, carry):
            c_copy(dz).wait_recv()
            fill([plus(ci, 1, cs) * zs + source_z(dz)], 0, group_rows // tile)
            return carry

        lax.fori_loop(1, zs, own_men, 0)
        lax.fori_loop(1, nm, other_men, 0)
        if cs > 1:
            lax.fori_loop(0, zs, other_core, 0)

    xy_sends = [(k, peer) for k, peer in enumerate(xy_ids)]
    zc_sends = [(dc * zs + send_order[n], zc_peer(dc, send_order[n]))
                for n in reversed(range(zs)) for dc in range(cs) if n + dc]

    def group_start(value, buf, me, send, recv, peers):
        buf[me] = value.astype(buf.dtype)
        copies = []
        for k, peer in peers:
            copy = remote(buf.at[me], buf.at[me], send.at[k], recv.at[k], peer)
            copy.start()
            copies.append(copy)
        pending.extend(copies)
        return copies

    def group_finish(copies, buf):
        for copy in copies:
            copy.wait_recv()
        total = buf[0].astype(F32)
        for slot in range(1, buf.shape[0]):
            total = total + buf[slot].astype(F32)
        return total

    def group_sum(value, buf, me, send, recv, peers):
        return group_finish(group_start(value, buf, me, send, recv, peers), buf)

    for copy in mass_copies:
        copy.wait_recv()
    men_mass = jnp.concatenate([mass_buf[x] for x in range(xs)], axis=1)
    men_full = jnp.concatenate([men_buf[k] for k in range(nm)], axis=1)
    mass_q = None
    for x in range(xs):
        order = [(z * xs + x) * cs + c for c in range(cs) for z in range(zs)]
        mine = jnp.concatenate([wm_ref[:, p * wb:(p + 1) * wb] for p in order], axis=0)
        mass_q = mine if mass_q is None else jnp.where(xi == x, mine, mass_q)

    def men_update(it, row_sum):
        return men_mass / group_sum(row_sum, r_buf.at[it], xy_me, rx_s.at[it], rx_r.at[it], xy_sends)

    def women_start(it, partial):
        return group_start(partial, c_buf.at[it], zc_me, cz_s.at[it], cz_r.at[it], zc_sends)

    def women_finish(it, copies):
        return mass_q / group_finish(copies, c_buf.at[it])

    zeros13 = jnp.zeros((13, group_rows), BF16)
    zeros13w = jnp.zeros((13, wb), BF16)

    def sweep(step, carry):
        for q in range(nb):
            carry = step(q, carry)
        return carry

    sums = rsum_ref[...]
    high = sums.astype(BF16)
    low = (sums - high.astype(F32)).astype(BF16)
    total = lax.dot_general(jnp.ones((16, 2 * lanes), BF16), jnp.concatenate([high, low], axis=1),
                            RHS_T, preferred_element_type=F32)
    scale = men_update(0, total[0:1])

    def col_sweep(scale):
        left = jnp.concatenate(list(split3(scale)) + [zeros13], axis=0)
        for q in range(nb):
            out = jnp.dot(left, e_ref[q], preferred_element_type=F32)
            col_ref[q:q + 1, :] = out[0:1] + out[1:2] + out[2:3]
        return col_ref[...]

    sums = col_sweep(scale)
    sent = women_start(0, sums)
    col_ref[...] = women_finish(0, sent)

    def row_step(q, total):
        lines = jnp.concatenate(list(split3(col_ref[q:q + 1, :])) + [zeros13w], axis=0)
        return total + lax.dot_general(lines, e_ref[q], RHS_T, preferred_element_type=F32)

    total = sweep(row_step, jnp.zeros((16, group_rows), F32))
    scale = men_update(1, total[0:1] + total[1:2] + total[2:3])
    sums = col_sweep(scale)
    sent = women_start(1, sums)
    for x in range(xs):
        scale_ref[x] = scale[:, x * rows:(x + 1) * rows]
    ms_out[...] = scale_ref[xi]
    weighted = (men_full.astype(F32) * scale).astype(BF16)
    share = traits // cs
    for q in range(nb):
        out = jnp.dot(weighted, e_ref[q], preferred_element_type=F32)
        for part in range(cs):
            t_ref[part, q] = out[part * share:(part + 1) * share]
    swaps = []
    if cs > 1:
        copy = remote(t_ref.at[plus(ci, 1, cs)], t_in, tx_s.at[0], tx_r.at[0], zc_peer(1, 0))
        copy.start()
        swaps.append(copy)
    pending.extend(swaps)
    women_scale = women_finish(1, sent)
    col_ref[...] = women_scale
    wx_buf[xi] = women_scale
    wx_copies = []
    for k, peer in enumerate(x_ids):
        copy = remote(wx_buf.at[xi], wx_buf.at[xi], wx_s.at[k], wx_r.at[k], peer)
        copy.start()
        wx_copies.append(copy)
    pending.extend(wx_copies)

    for copy in swaps:
        copy.wait_recv()

    def moment_step(q, moment):
        inner = t_ref[ci, q]
        if cs > 1:
            inner = inner + t_in[q]
        inner = inner * col_ref[q:q + 1, :]
        high = inner.astype(BF16)
        low = (inner - high.astype(F32)).astype(BF16)
        both = jnp.concatenate([high, low], axis=0)
        return moment + lax.dot_general(both, wom_buf[q, 0:traits], RHS_T, preferred_element_type=F32)

    moment = sweep(moment_step, jnp.zeros((2 * share, traits), F32))
    moment = moment[0:share] + moment[share:]
    half = share // 2
    packed = jnp.concatenate([moment[0:half], moment[half:]], axis=1)
    packed = group_sum(packed, mxy_buf, xy_me, rx_s.at[2], rx_r.at[2], xy_sends)
    sent = group_start(packed, mz_buf, zc_me, mz_s, mz_r, zc_sends)
    for copy in wx_copies:
        copy.wait_recv()
    for x in range(xs):
        scales = wx_buf[x]
        for q in range(nb):
            p = ((q % zs) * xs + x) * cs + q // zs
            ws_out[:, p * wb:(p + 1) * wb] = scales[q:q + 1, :]
    for copy in sent:
        copy.wait_recv()
    parts = []
    for part in range(cs):
        packed = mz_buf[part * zs]
        for z in range(1, zs):
            packed = packed + mz_buf[part * zs + z]
        parts += [packed[:, 0:traits], packed[:, traits:]]
    moment = jnp.concatenate(parts, axis=0)
    up_out[...] = aff_ref[...] + obs_ref[...] - moment * (1.0 / men_total)

    for copy in pending:
        copy.wait_send()
    for dz in range(1, zs):
        z_copy(dz).wait_send()
    for k in range(1, nm):
        m_copy(k).wait_send()
    if cs > 1:
        for dz in range(zs):
            c_copy(dz).wait_send()


def deliver(ms_ref, ws_ref, up_ref, ms_out, ws_out, up_out, sems):
    copies = [
        pltpu.make_async_copy(src, dst, sems.at[k])
        for k, (src, dst) in enumerate([(ms_ref, ms_out), (ws_ref, ws_out), (up_ref, up_out)])
    ]
    for copy in copies:
        copy.start()
    for copy in copies:
        copy.wait()


def solution(mesh):
    men_axis, women_axis = mesh.shape["men"], mesh.shape["women"]
    dims = factors(men_axis)
    zs, xs, cs = dims

    def on_device(men_traits, women_traits, affinity, observed, men_mass, women_mass):
        traits, mb = men_traits.shape
        wb = women_traits.shape[1]
        rows, cols = men_mass.shape[0], women_mass.shape[0]
        nm, nb = xs * women_axis, zs * cs
        deep = traits + 16
        dma = pltpu.SemaphoreType.DMA
        vmem = pl.BlockSpec(memory_space=pltpu.VMEM)
        anywhere = pl.BlockSpec(memory_space=pl.ANY)
        packed = (traits // cs // 2, 2 * traits)
        out = pl.pallas_call(
            functools.partial(body, dims, women_axis, rows * men_axis, cols * women_axis),
            out_shape=(
                pltpu.VMEM((1, rows), F32),
                pltpu.VMEM((1, cols), F32),
                pltpu.VMEM((traits, traits), F32),
            ),
            in_specs=[anywhere] * 6,
            out_specs=(vmem, vmem, vmem),
            scratch_shapes=[
                pltpu.VMEM((nm, traits, mb), BF16),
                pltpu.VMEM((nb, deep, wb), BF16),
                pltpu.VMEM((nm * mb, deep), BF16),
                pltpu.VMEM((nb, nm * mb, wb), BF16),
                pltpu.VMEM((cs, nb, traits // cs, wb), F32),
                pltpu.VMEM((nb, wb), F32),
                pltpu.VMEM((nm * mb, wb if wb % 128 else 128), F32),
                pltpu.VMEM((xs, 1, rows), F32),
                pltpu.VMEM((deep, 3 * traits), BF16),
                pltpu.VMEM((traits, traits), F32),
                pltpu.VMEM((traits, traits), F32),
                pltpu.VMEM((1, cols), F32),
                pltpu.VMEM((xs, 1, rows), F32),
                pltpu.VMEM((xs, nb, wb), F32),
                pltpu.VMEM((2, nm, 1, nm * mb), F32),
                pltpu.VMEM((2, nb, nb, wb), BF16),
                pltpu.VMEM((nm,) + packed, F32),
                pltpu.VMEM((nb,) + packed, F32),
                pltpu.VMEM((nb, traits // cs, wb), F32),
                dma((6,)),
                dma((nm,)), dma((nm,)),
                dma((zs,)), dma((zs,)),
                dma((zs,)), dma((zs,)),
                dma((xs,)), dma((xs,)),
                dma((xs,)), dma((xs,)),
                dma((3, nm)), dma((3, nm)),
                dma((2, nb)), dma((2, nb)),
                dma((1,)), dma((1,)),
                dma((nb,)), dma((nb,)),
            ],
            compiler_params=pltpu.CompilerParams(
                collective_id=0, has_side_effects=True, vmem_limit_bytes=60 * 1024 * 1024),
        )(men_traits, women_traits, affinity, observed,
          men_mass.reshape(1, rows), women_mass.reshape(1, cols))
        out = pl.pallas_call(
            deliver,
            out_shape=(
                jax.ShapeDtypeStruct((1, rows), F32),
                jax.ShapeDtypeStruct((1, cols), F32),
                jax.ShapeDtypeStruct((traits, traits), F32),
            ),
            in_specs=[vmem] * 3,
            out_specs=(anywhere,) * 3,
            scratch_shapes=[dma((3,))],
        )(*[pltpu.with_memory_space_constraint(value, pltpu.VMEM) for value in out])
        return out[0].reshape(rows), out[1].reshape(cols), out[2]

    placed = (P(None, ("men", "women")), P(None, ("women", "men")), P(), P(), P("men"), P("women"))
    return jax.shard_map(
        on_device,
        mesh=mesh,
        in_specs=placed,
        out_specs=(P("men"), P("women"), P()),
        check_vma=False,
    )
```

```python
import functools
import math
import jax
import jax.numpy as jnp
import ml_dtypes
import numpy as np
from jax import lax
from jax.experimental import pallas as pl
from jax.experimental.pallas import tpu as pltpu
from jax.sharding import PartitionSpec as P

F32, BF16 = jnp.float32, jnp.bfloat16
MESH = pl.DeviceIdType.MESH
LHS_T = (((0,), (0,)), ((), ()))
RHS_T = (((1,), (1,)), ((), ()))


def split3(value):
    high = value.astype(BF16)
    rest = value - high.astype(F32)
    mid = rest.astype(BF16)
    low = (rest - mid.astype(F32)).astype(BF16)
    return high, mid, low


def factors(men):
    cores = 2 if men % 2 == 0 else 1
    chips = men // cores
    planes = 1 << (chips.bit_length() // 2)
    if chips % planes:
        planes = 1
    return planes, chips // planes, cores


def body(dims, ws, men_total, women_total,
         men_ref, women_ref, aff_hbm, obs_hbm, mm_hbm, wm_hbm,
         ms_out, ws_out, up_out,
         men_buf, wom_buf, scaled_ref, tall_ref, e_ref, et_ref, t_ref, col_ref, rsum_ref, scale_ref,
         left_aff, aff_ref, obs_ref, wm_ref, mass_buf, wx_buf,
         r_buf, c_buf, mxy_buf, mz_buf, t_in,
         own_sem, gm_s, gm_r, gz_s, gz_r, gc_s, gc_r, mm_s, mm_r, wx_s, wx_r,
         rx_s, rx_r, cz_s, cz_r, tx_s, tx_r, mz_s, mz_r):
    zs, xs, cs = dims
    nm, nb = xs * ws, zs * cs
    traits, wb = women_ref.shape
    deep = wom_buf.shape[1]
    mb = men_ref.shape[1]
    rows = mm_hbm.shape[1]
    group_rows = nm * mb
    log_count = math.log(women_total)
    mi = lax.axis_index("men")
    yi = lax.axis_index("women")
    ci = lax.rem(mi, cs)
    xi = lax.rem(lax.div(mi, cs), xs)
    zi = lax.div(mi, cs * xs)
    xy_me = xi * ws + yi
    zc_me = ci * zs + zi

    def plus(value, step, size):
        return lax.rem(value + step, size)

    def xy_peer(dx, dy):
        return ((zi * xs + plus(xi, dx, xs)) * cs + ci, plus(yi, dy, ws))

    def zc_peer(dc, dz):
        return ((plus(zi, dz, zs) * xs + xi) * cs + plus(ci, dc, cs), yi)

    def traits_of(q):
        return wom_buf.at[q, pl.ds(0, traits)]

    xy_ids = [xy_peer(dx, dy) for dx in range(xs) for dy in range(ws) if dx + dy]
    zc_ids = [zc_peer(dc, dz) for dc in range(cs) for dz in range(zs) if dc + dz]
    x_ids = [xy_peer(dx, 0) for dx in range(1, xs)]

    barrier = pltpu.get_barrier_semaphore()
    everyone = xy_ids + zc_ids
    for peer in everyone:
        pl.semaphore_signal(barrier, inc=1, device_id=peer, device_id_type=MESH)
    local = [
        pltpu.make_async_copy(src, dst, own_sem.at[k])
        for k, (src, dst) in enumerate([
            (men_ref, men_buf.at[xy_me]), (women_ref, traits_of(zc_me)), (aff_hbm, aff_ref),
            (mm_hbm, mass_buf.at[xi]), (wm_hbm, wm_ref), (obs_hbm, obs_ref)])
    ]
    for copy in local:
        copy.start()
    def remote(src, dst, send, recv, peer):
        return pltpu.make_async_remote_copy(
            src_ref=src, dst_ref=dst, send_sem=send, recv_sem=recv,
            device_id=peer, device_id_type=MESH)

    def z_copy(dz):
        return remote(traits_of(zc_me), traits_of(zc_me), gz_s.at[dz], gz_r.at[dz], zc_peer(0, dz))

    def source_z(dz):
        return plus(zi, zs - dz, zs)

    def c_copy(dz):
        held = traits_of(ci * zs + source_z(dz))
        return remote(held, held, gc_s.at[dz], gc_r.at[dz], zc_peer(1, 0))

    def m_copy(k):
        return remote(men_buf.at[xy_me], men_buf.at[xy_me], gm_s.at[k], gm_r.at[k],
                      xy_peer(lax.div(k, ws), lax.rem(k, ws)))

    def by_distance(sign):
        order = [0]
        for n in range(1, zs):
            near = [sorted(range(zs), key=lambda z: (abs(z - own), -z))[n] for own in range(zs)]
            steps = [sign * (z - own) % zs for own, z in enumerate(near)]
            value = jnp.int32(steps[0])
            for own in range(1, zs):
                value = jnp.where(zi == own, steps[own], value)
            order.append(value)
        return order

    order, send_order = by_distance(-1), by_distance(1)
    first_copy = remote(traits_of(zc_me), traits_of(zc_me), gc_s.at[0], gc_r.at[0], zc_peer(1, 0)) if cs > 1 else None
    pl.semaphore_wait(barrier, len(everyone))
    local[0].wait()
    local[1].wait()
    if cs > 1:
        first_copy.start()
    for n in range(1, zs):
        z_copy(send_order[n]).start()
    late = [nm - 1] if cs == 2 and nm == 4 and zs == 4 else []
    for k in range(1, nm - len(late)):
        m_copy(k).start()
    pending = []
    for k, peer in enumerate(x_ids):
        copy = remote(mm_hbm, mass_buf.at[xi], mm_s.at[k], mm_r.at[k], peer)
        copy.start()
        pending.append(copy)
    mass_copies = list(pending)

    def shard_of(k):
        return plus(xi, xs - lax.div(k, ws), xs) * ws + plus(yi, ws - lax.rem(k, ws), ws)

    def rows_of(shard):
        return pl.ds(pl.multiple_of(shard * mb, mb), mb)

    tile = math.gcd(mb, 256)
    fold = wb // 128 if wb % 128 == 0 else 1
    lanes = wb // fold

    def make_scaled(shard):
        block = men_buf[shard]
        tall = jnp.dot(left_aff[...], jnp.concatenate([block] * 3, axis=0), preferred_element_type=F32)
        tall = tall + ones_column
        tall_ref[shard] = tall.astype(BF16)
        scaled_ref[rows_of(shard), :] = jnp.transpose(tall).astype(BF16)

    def fill(blocks, start, count):
        for part in range(count):
            at = pl.ds(pl.multiple_of(start + part * tile, tile), tile)
            total = None
            for q in blocks:
                surplus = jnp.dot(scaled_ref[at, :], wom_buf[q], preferred_element_type=F32)
                kernel = jnp.exp(surplus)
                e_ref[q, at, :] = kernel.astype(BF16)
                for piece in range(fold):
                    term = kernel[:, piece * lanes:(piece + 1) * lanes]
                    total = term if total is None else total + term
            rsum_ref[at, :] += total

    def fill_men(blocks, ks):
        for k in ks:
            fill(blocks, shard_of(k) * mb, mb // tile)

    place = lax.broadcasted_iota(jnp.int32, (deep, 1), 0)
    ones_column = jnp.where((place >= traits) & (place < traits + 3), 1.0, 0.0).astype(F32)
    line = lax.broadcasted_iota(jnp.int32, (deep - traits, wb), 0)
    tail = jnp.zeros((deep - traits, wb), F32)
    rest = log_count
    for step in range(3):
        piece = float(np.asarray(rest, ml_dtypes.bfloat16))
        tail = jnp.where(line == step, -piece, tail)
        rest -= piece
    tail = tail.astype(BF16)
    for q in range(nb):
        wom_buf[q, traits:] = tail
    rsum_ref[...] = jnp.zeros_like(rsum_ref)
    for copy in local[2:]:
        copy.wait()
    wide = jnp.concatenate(split3(jnp.transpose(aff_ref[...])), axis=1)
    left_aff[...] = jnp.concatenate([wide, jnp.zeros((deep - traits, 3 * traits), BF16)], axis=0)
    make_scaled(xy_me)
    fill([zc_me], xy_me * mb, mb // tile)

    def own_block(n):
        return ci * zs + source_z(order[n])

    def twin_block(n):
        return plus(ci, 1, cs) * zs + source_z(order[n])

    if cs == 2 and nm == 4 and zs == 4:
        def take_z(n):
            z_copy(order[n]).wait_recv()
            c_copy(order[n]).start()

        def cells(blocks, ks):
            for k in ks:
                fill(blocks, shard_of(k) * mb, mb // tile)

        c_copy(0).wait_recv()
        cells([twin_block(0)], [0])
        m_copy(3).start()
        take_z(1)
        cells([own_block(1)], [0])
        m_copy(2).wait_recv()
        take_z(2)
        cells([own_block(2)], [0])
        make_scaled(shard_of(2))
        c_copy(order[1]).wait_recv()
        m_copy(1).wait_recv()
        early = [own_block(0), twin_block(0), own_block(1), own_block(2), twin_block(1)]
        cells(early, [2])
        cells([twin_block(1)], [0])
        make_scaled(shard_of(1))
        take_z(3)
        m_copy(3).wait_recv()
        cells(early + [own_block(3)], [1])
        cells([own_block(3)], [0, 2])
        make_scaled(shard_of(3))
        c_copy(order[2]).wait_recv()
        cells(early + [own_block(3), twin_block(2)], [3])
        cells([twin_block(2)], [0, 1, 2])
        c_copy(order[3]).wait_recv()
        fill([twin_block(3)], 0, group_rows // tile)
    else:
        def own_men(dz, carry):
            z_copy(dz).wait_recv()
            if cs > 1:
                c_copy(dz).start()
            fill([ci * zs + source_z(dz)], xy_me * mb, mb // tile)
            return carry

        def other_men(k, carry):
            m_copy(k).wait_recv()
            shard = shard_of(k)
            make_scaled(shard)
            for z in range(zs):
                fill([ci * zs + z], shard * mb, mb // tile)
            return carry

        def other_core(dz, carry):
            c_copy(dz).wait_recv()
            fill([plus(ci, 1, cs) * zs + source_z(dz)], 0, group_rows // tile)
            return carry

        lax.fori_loop(1, zs, own_men, 0)
        lax.fori_loop(1, nm, other_men, 0)
        if cs > 1:
            lax.fori_loop(0, zs, other_core, 0)

    xy_sends = [(k, peer) for k, peer in enumerate(xy_ids)][::-1]
    zc_sends = [(dc * zs + send_order[n], zc_peer(dc, send_order[n]))
                for n in reversed(range(zs)) for dc in range(cs) if n + dc]

    def group_start(value, buf, me, send, recv, peers):
        buf[me] = value.astype(buf.dtype)
        copies = []
        for k, peer in peers:
            copy = remote(buf.at[me], buf.at[me], send.at[k], recv.at[k], peer)
            copy.start()
            copies.append(copy)
        pending.extend(copies)
        return copies

    def group_finish(copies, buf):
        for copy in copies:
            copy.wait_recv()
        total = buf[0].astype(F32)
        for slot in range(1, buf.shape[0]):
            total = total + buf[slot].astype(F32)
        return total

    def group_sum(value, buf, me, send, recv, peers):
        return group_finish(group_start(value, buf, me, send, recv, peers), buf)

    for copy in mass_copies:
        copy.wait_recv()
    men_mass = jnp.concatenate([mass_buf[x] for x in range(xs)], axis=1)
    men_full = jnp.concatenate([men_buf[k] for k in range(nm)], axis=1)
    mass_q = None
    for x in range(xs):
        order = [(z * xs + x) * cs + c for c in range(cs) for z in range(zs)]
        mine = jnp.concatenate([wm_ref[:, p * wb:(p + 1) * wb] for p in order], axis=0)
        mass_q = mine if mass_q is None else jnp.where(xi == x, mine, mass_q)

    def men_start(it, row_sum):
        return group_start(row_sum, r_buf.at[it], xy_me, rx_s.at[it], rx_r.at[it], xy_sends)

    def men_finish(it, copies):
        return men_mass / group_finish(copies, r_buf.at[it])

    def mirror(first, last):
        def one(q, carry):
            block = jnp.transpose(wom_buf[q].astype(F32)).astype(BF16)
            at = pl.ds(pl.multiple_of(q * wb, wb), wb)
            for k in range(nm):
                surplus = jnp.dot(block, tall_ref[k], preferred_element_type=F32)
                et_ref[k, at, :] = jnp.exp(surplus).astype(BF16)
            return carry

        lax.fori_loop(first, last, one, 0)

    def women_start(it, partial):
        return group_start(partial, c_buf.at[it], zc_me, cz_s.at[it], cz_r.at[it], zc_sends)

    def women_finish(it, copies):
        return mass_q / group_finish(copies, c_buf.at[it])

    zeros13 = jnp.zeros((13, group_rows), BF16)

    def sweep(step, carry):
        for q in range(nb):
            carry = step(q, carry)
        return carry

    sums = rsum_ref[...]
    high = sums.astype(BF16)
    low = (sums - high.astype(F32)).astype(BF16)
    total = lax.dot_general(jnp.ones((16, 2 * lanes), BF16), jnp.concatenate([high, low], axis=1),
                            RHS_T, preferred_element_type=F32)
    sent = men_start(0, total[0:1])
    mirror(0, 3 * nb // 8)
    scale = men_finish(0, sent)

    def col_sweep(scale):
        left = jnp.concatenate(list(split3(scale)) + [zeros13], axis=0)
        for q in range(nb):
            out = jnp.dot(left, e_ref[q], preferred_element_type=F32)
            col_ref[q:q + 1, :] = out[0:1] + out[1:2] + out[2:3]
        return col_ref[...]

    sums = col_sweep(scale)
    sent = women_start(0, sums)
    mirror(3 * nb // 8, nb)
    women_scale = women_finish(0, sent)

    spread = jnp.concatenate([women_scale[q:q + 1] for q in range(nb)], axis=1)
    lines = jnp.concatenate(list(split3(spread)) + [jnp.zeros((13, nb * wb), BF16)], axis=0)
    total = jnp.concatenate(
        [jnp.dot(lines, et_ref[k], preferred_element_type=F32) for k in range(nm)], axis=1)
    sent = men_start(1, total[0:1] + total[1:2] + total[2:3])
    scale = men_finish(1, sent)
    sums = col_sweep(scale)
    sent = women_start(1, sums)
    for x in range(xs):
        scale_ref[x] = scale[:, x * rows:(x + 1) * rows]
    ms_out[...] = scale_ref[xi]
    weighted = (men_full.astype(F32) * scale).astype(BF16)
    share = traits // cs
    for q in range(nb):
        out = jnp.dot(weighted, e_ref[q], preferred_element_type=F32)
        for part in range(cs):
            t_ref[part, q] = out[part * share:(part + 1) * share]
    swaps = []
    if cs > 1:
        copy = remote(t_ref.at[plus(ci, 1, cs)], t_in, tx_s.at[0], tx_r.at[0], zc_peer(1, 0))
        copy.start()
        swaps.append(copy)
    pending.extend(swaps)
    women_scale = women_finish(1, sent)
    col_ref[...] = women_scale
    wx_buf[xi] = women_scale
    wx_copies = []
    for k, peer in enumerate(x_ids):
        copy = remote(wx_buf.at[xi], wx_buf.at[xi], wx_s.at[k], wx_r.at[k], peer)
        copy.start()
        wx_copies.append(copy)
    pending.extend(wx_copies)

    for copy in swaps:
        copy.wait_recv()

    def moment_step(q, moment):
        inner = t_ref[ci, q]
        if cs > 1:
            inner = inner + t_in[q]
        inner = inner * col_ref[q:q + 1, :]
        high = inner.astype(BF16)
        low = (inner - high.astype(F32)).astype(BF16)
        both = jnp.concatenate([high, low], axis=0)
        return moment + lax.dot_general(both, wom_buf[q, 0:traits], RHS_T, preferred_element_type=F32)

    moment = sweep(moment_step, jnp.zeros((2 * share, traits), F32))
    moment = moment[0:share] + moment[share:]
    half = share // 2
    packed = jnp.concatenate([moment[0:half], moment[half:]], axis=1)
    packed = group_sum(packed, mxy_buf, xy_me, rx_s.at[2], rx_r.at[2], xy_sends)
    sent = group_start(packed, mz_buf, zc_me, mz_s, mz_r, zc_sends)
    for copy in wx_copies:
        copy.wait_recv()
    for x in range(xs):
        scales = wx_buf[x]
        for q in range(nb):
            p = ((q % zs) * xs + x) * cs + q // zs
            ws_out[:, p * wb:(p + 1) * wb] = scales[q:q + 1, :]
    for copy in sent:
        copy.wait_recv()
    parts = []
    for part in range(cs):
        packed = mz_buf[part * zs]
        for z in range(1, zs):
            packed = packed + mz_buf[part * zs + z]
        parts += [packed[:, 0:traits], packed[:, traits:]]
    moment = jnp.concatenate(parts, axis=0)
    up_out[...] = aff_ref[...] + obs_ref[...] - moment * (1.0 / men_total)

    for copy in pending:
        copy.wait_send()
    for dz in range(1, zs):
        z_copy(dz).wait_send()
    for k in range(1, nm):
        m_copy(k).wait_send()
    if cs > 1:
        for dz in range(zs):
            c_copy(dz).wait_send()


def deliver(ms_ref, ws_ref, up_ref, ms_out, ws_out, up_out, sems):
    copies = [
        pltpu.make_async_copy(src, dst, sems.at[k])
        for k, (src, dst) in enumerate([(ms_ref, ms_out), (ws_ref, ws_out), (up_ref, up_out)])
    ]
    for copy in copies:
        copy.start()
    for copy in copies:
        copy.wait()


def solution(mesh):
    men_axis, women_axis = mesh.shape["men"], mesh.shape["women"]
    dims = factors(men_axis)
    zs, xs, cs = dims

    def on_device(men_traits, women_traits, affinity, observed, men_mass, women_mass):
        traits, mb = men_traits.shape
        wb = women_traits.shape[1]
        rows, cols = men_mass.shape[0], women_mass.shape[0]
        nm, nb = xs * women_axis, zs * cs
        deep = traits + 16
        dma = pltpu.SemaphoreType.DMA
        vmem = pl.BlockSpec(memory_space=pltpu.VMEM)
        anywhere = pl.BlockSpec(memory_space=pl.ANY)
        packed = (traits // cs // 2, 2 * traits)
        out = pl.pallas_call(
            functools.partial(body, dims, women_axis, rows * men_axis, cols * women_axis),
            out_shape=(
                pltpu.VMEM((1, rows), F32),
                pltpu.VMEM((1, cols), F32),
                pltpu.VMEM((traits, traits), F32),
            ),
            in_specs=[anywhere] * 6,
            out_specs=(vmem, vmem, vmem),
            scratch_shapes=[
                pltpu.VMEM((nm, traits, mb), BF16),
                pltpu.VMEM((nb, deep, wb), BF16),
                pltpu.VMEM((nm * mb, deep), BF16),
                pltpu.VMEM((nm, deep, mb), BF16),
                pltpu.VMEM((nb, nm * mb, wb), BF16),
                pltpu.VMEM((nm, nb * wb, mb), BF16),
                pltpu.VMEM((cs, nb, traits // cs, wb), F32),
                pltpu.VMEM((nb, wb), F32),
                pltpu.VMEM((nm * mb, wb if wb % 128 else 128), F32),
                pltpu.VMEM((xs, 1, rows), F32),
                pltpu.VMEM((deep, 3 * traits), BF16),
                pltpu.VMEM((traits, traits), F32),
                pltpu.VMEM((traits, traits), F32),
                pltpu.VMEM((1, cols), F32),
                pltpu.VMEM((xs, 1, rows), F32),
                pltpu.VMEM((xs, nb, wb), F32),
                pltpu.VMEM((2, nm, 1, nm * mb), F32),
                pltpu.VMEM((2, nb, nb, wb), BF16),
                pltpu.VMEM((nm,) + packed, F32),
                pltpu.VMEM((nb,) + packed, F32),
                pltpu.VMEM((nb, traits // cs, wb), F32),
                dma((6,)),
                dma((nm,)), dma((nm,)),
                dma((zs,)), dma((zs,)),
                dma((zs,)), dma((zs,)),
                dma((xs,)), dma((xs,)),
                dma((xs,)), dma((xs,)),
                dma((3, nm)), dma((3, nm)),
                dma((2, nb)), dma((2, nb)),
                dma((1,)), dma((1,)),
                dma((nb,)), dma((nb,)),
            ],
            compiler_params=pltpu.CompilerParams(
                collective_id=0, has_side_effects=True, vmem_limit_bytes=60 * 1024 * 1024),
        )(men_traits, women_traits, affinity, observed,
          men_mass.reshape(1, rows), women_mass.reshape(1, cols))
        out = pl.pallas_call(
            deliver,
            out_shape=(
                jax.ShapeDtypeStruct((1, rows), F32),
                jax.ShapeDtypeStruct((1, cols), F32),
                jax.ShapeDtypeStruct((traits, traits), F32),
            ),
            in_specs=[vmem] * 3,
            out_specs=(anywhere,) * 3,
            scratch_shapes=[dma((3,))],
        )(*[pltpu.with_memory_space_constraint(value, pltpu.VMEM) for value in out])
        return out[0].reshape(rows), out[1].reshape(cols), out[2]

    placed = (P(None, ("men", "women")), P(None, ("women", "men")), P(), P(), P("men"), P("women"))
    return jax.shard_map(
        on_device,
        mesh=mesh,
        in_specs=placed,
        out_specs=(P("men"), P("women"), P()),
        check_vma=False,
    )
```
